256 devices in a mesh: mom: 32 (over x, z), tm: 8 (over y, core).
Axes of the slice: x: 4, y: 4, z: 8, core: 2. Of those that a mesh axis runs over, the one named last changes fastest.
Arguments:
- green: bfloat16 [64, 32, 128, 2048], P('mom', None, None, 'tm'), may hold values from -6 to 6
- hole: bfloat16 [64, 32, 128, 2048], P('mom', None, None, 'tm'), may hold values from -6 to 6
- decay_log: float32 [64, 8, 2048], P('mom', None, 'tm'), as said below
- phase_step: float32 [64, 8, 2048], P('mom', None, 'tm'), may hold values from -1 to 1
Outputs:
- collision: bfloat16 [64, 32, 128, 2048], P('mom', None, None, 'tm')
The draws below stay inside these ranges and needn't reach their ends.
Inputs may be any that keep to these rules, and one draw needn't show every extreme that they name: decay_log holds logarithms of decay factors of at most one.
All inputs are finite; a program needn't handle non-finite values.
Results may differ from the reference program's by a relative error of at most 0.0067.
Values may be sent and summed in bfloat16 or wider, within the bound.
A program may use at most 128 MiB of HBM per device.

```python
import math
import jax
import jax.numpy as jnp
from jax import lax

MOMENTA = 64
ORBITALS = 8
FIELD = 128
ROWS = 32
MEMORY_SLICES = 2048


def draw_decay_log(key, part):
    stochastic_seeds = jax.random.split(key, 6)
    chooser = jax.random.randint(stochastic_seeds[0], (MOMENTA, ORBITALS, 1), 0, 2)
    slow_mask = chooser == 1
    slow_rate = jnp.exp(jax.random.uniform(stochastic_seeds[1], (MOMENTA, ORBITALS, 1), jnp.float32, math.log(0.1 / MEMORY_SLICES), math.log(1.0 / MEMORY_SLICES)))
    fast_rate = jnp.exp(jax.random.uniform(stochastic_seeds[2], (MOMENTA, ORBITALS, 1), jnp.float32, math.log(1.0 / 50.0), math.log(1.0 / 30.0)))
    steady_damping = jnp.where(slow_mask, slow_rate, fast_rate)
    stochastic_jitter = jax.random.uniform(stochastic_seeds[3], (MOMENTA, ORBITALS, MEMORY_SLICES), jnp.float32, 0.5, 1.5)
    spike_location = jax.random.randint(stochastic_seeds[4], (3,), 0, MEMORY_SLICES)
    memory_lengths = jax.random.uniform(stochastic_seeds[5], (3,), jnp.float32, math.log(0.5), math.log(0.8))
    slice_ordinal = jnp.arange(MEMORY_SLICES, dtype=jnp.int32)
    spike_occurrences = jnp.sum(jnp.where(slice_ordinal[None, :] == spike_location[:, None], memory_lengths[:, None], 0.0), axis=0)
    return -steady_damping * stochastic_jitter + spike_occurrences[None, None, :]


def levels(rng, shape, cuts, smallest, largest):
    gain, own = 1.0, jax.random.fold_in(rng, 6)
    for dim, blocks in cuts:
        draws = jnp.exp(jax.random.uniform(jax.random.fold_in(own, dim), (blocks,), jnp.float32, smallest / len(cuts), largest / len(cuts)))
        gain = gain * jnp.repeat(draws, shape[dim] // blocks).reshape([-1 if axis == dim else 1 for axis in range(len(shape))])
    return gain


def normal_values(key, dims, scale, limit, cuts=(), kind=jnp.bfloat16):
    factor_of = levels(key, dims, cuts, -0.22, 0.18) if cuts else 1.0
    entries = jax.random.normal(key, dims, jnp.float32) * scale * factor_of
    return jnp.minimum(jnp.maximum(entries, -limit), limit).astype(kind)


def setup_inputs(seed: int = 0) -> dict:
    keys = jax.random.split(jax.random.key(seed), 5)
    return {
        "green": normal_values(keys[0], (MOMENTA, ROWS, FIELD, MEMORY_SLICES), 1.0, 6.0, ((0, 32), (3, 8))),
        "hole": normal_values(keys[1], (MOMENTA, ROWS, FIELD, MEMORY_SLICES), 1.0, 6.0, ((0, 32), (3, 8))),
        "decay_log": draw_decay_log(jax.random.fold_in(keys[4], 71), 0),
        "phase_step": jnp.clip(jax.random.uniform(keys[3], (MOMENTA, ORBITALS, MEMORY_SLICES), jnp.float32, -1.0, 1.0) * levels(keys[3], (MOMENTA, ORBITALS, MEMORY_SLICES), ((0, 32), (2, 8)), -0.4, 0.0), -1.0, 1.0),
    }


step_weight = 0.0625
coupling = 0.25

def transform_matrix(handed):
    numbers = jnp.arange(MOMENTA, dtype=jnp.int32)
    product = numbers[:, None] * numbers[None, :] % MOMENTA
    angles = product.astype(jnp.float32) * (2.0 * math.pi / MOMENTA)
    scaled = 1.0 / math.sqrt(MOMENTA)
    cosine = (jnp.cos(angles) * scaled).astype(jnp.bfloat16)
    sine = (handed * jnp.sin(angles) * scaled).astype(jnp.bfloat16)
    upper = jnp.stack([cosine, -sine], axis=-1)
    lower = jnp.stack([sine, cosine], axis=-1)
    return jnp.stack([upper, lower], axis=1)

def transform(matrix, field):
    return jnp.einsum('rokI,kpIC->rpoC', matrix.astype(jnp.float32), field.astype(jnp.float32), precision=lax.Precision.HIGHEST)

def self_energy(green_space, hole_space):
    green_re = green_space[:, :, 0, :]
    green_im = green_space[:, :, 1, :]
    hole_re = hole_space[:, :, 0, :]
    hole_im = hole_space[:, :, 1, :]
    square_re = green_re * green_re - green_im * green_im
    square_im = 2.0 * green_re * green_im
    energy_re = coupling * (square_re * hole_re - square_im * hole_im)
    energy_im = coupling * (square_re * hole_im + square_im * hole_re)
    return jnp.stack([energy_re, energy_im], axis=2).astype(jnp.bfloat16)

def reference(green, hole, decay_log, phase_step):
    plus = transform_matrix(1.0)
    minus = transform_matrix(-1.0)
    shrink = jnp.moveaxis(jnp.exp(decay_log), -1, 0)
    cosine = jnp.moveaxis(jnp.cos(phase_step), -1, 0)
    sine = jnp.moveaxis(jnp.sin(phase_step), -1, 0)
    pairs = ORBITALS * ORBITALS

    def one_row(row_index):
        green_row = lax.dynamic_index_in_dim(green, row_index, 1, keepdims=False)
        hole_row = lax.dynamic_index_in_dim(hole, row_index, 1, keepdims=False)
        green_split = green_row.reshape(MOMENTA, pairs, 2, MEMORY_SLICES)
        hole_split = hole_row.reshape(MOMENTA, pairs, 2, MEMORY_SLICES)
        green_space = transform(plus, green_split)
        hole_space = transform(minus, hole_split)
        sigma_space = self_energy(green_space, hole_space)
        sigma = transform(minus, sigma_space)
        sigma_cols = jnp.moveaxis(sigma.reshape(MOMENTA, ORBITALS, ORBITALS, 2, MEMORY_SLICES), -1, 0)

        def advance(carried, column):
            source, factor, turn_cos, turn_sin = column
            factor_wide = factor[:, None, :]
            cos_wide = turn_cos[:, None, :]
            sin_wide = turn_sin[:, None, :]
            new_re = factor_wide * (cos_wide * carried[..., 0] - sin_wide * carried[..., 1]) + source[..., 0]
            new_im = factor_wide * (sin_wide * carried[..., 0] + cos_wide * carried[..., 1]) + source[..., 1]
            updated = jnp.stack([new_re, new_im], axis=-1)
            return (updated, updated)
        start = jnp.zeros((MOMENTA, ORBITALS, ORBITALS, 2), jnp.float32)
        _, history = lax.scan(advance, start, (sigma_cols, shrink, cosine, sine))
        weighted = step_weight * history
        return jnp.moveaxis(weighted, 0, -1).reshape(MOMENTA, FIELD, MEMORY_SLICES).astype(jnp.bfloat16)
    rows_out = lax.map(one_row, jnp.arange(ROWS, dtype=jnp.int32))
    return jnp.moveaxis(rows_out, 0, 1)
```

```python
import functools
import math

import jax
import jax.numpy as jnp
import numpy as np
from jax import lax
from jax.experimental import pallas as pl
from jax.experimental.pallas import tpu as pltpu
from jax.sharding import PartitionSpec as P

MESH = pl.DeviceIdType.MESH
F32 = jnp.float32
BF16 = jnp.bfloat16
MOMENTA = 64
ORBITALS = 8
WIDE = 2 * ORBITALS
COUPLING = 0.25
STEP_WEIGHT = 0.0625
LEVELS = 8
ROW_GROUP = 8


def transform_table(handed):
    numbers = np.arange(MOMENTA)
    product = (numbers[:, None] * numbers[None, :]) % MOMENTA
    angles = product.astype(np.float32) * np.float32(2.0 * math.pi / MOMENTA)
    scaled = np.float32(1.0 / math.sqrt(MOMENTA))
    cosine = np.cos(angles) * scaled
    sine = np.float32(handed) * np.sin(angles) * scaled
    return jnp.asarray(np.block([[cosine, -sine], [sine, cosine]]).astype(jnp.bfloat16))


def kernel(
    mom, tm, rows,
    green, hole, decay, phase, plus, minus,
    out,
    gh, sb, rb, tg, th, ts, coef, turn, grow, ends, local, wide, done,
    est, ebox, pst, pbox,
    fwd_send, fwd_recv, ret_send, ret_recv, end_send, end_recv, prod_send, prod_recv, out_sem,
):
    m = lax.axis_index("mom")
    n = lax.axis_index("tm")
    chunks = ORBITALS
    groups = 2 * rows // ROW_GROUP
    per_k = rows // ROW_GROUP

    def field(a):
        return pl.ds(pl.multiple_of(a * WIDE, WIDE), WIDE)

    barrier = pltpu.get_barrier_semaphore()
    ebox[...] = jnp.zeros_like(ebox)
    pbox[...] = jnp.zeros_like(pbox)

    def greet_mom(j, carry):
        pl.semaphore_signal(barrier, inc=1, device_id={"mom": lax.rem(m + j, mom)}, device_id_type=MESH)
        return carry

    def greet_tm(j, carry):
        pl.semaphore_signal(barrier, inc=1, device_id={"tm": lax.rem(n + j, tm)}, device_id_type=MESH)
        return carry

    lax.fori_loop(1, mom, greet_mom, 0)
    lax.fori_loop(1, tm, greet_tm, 0)
    pl.semaphore_wait(barrier, mom + tm - 2)

    def send_fields(a, carry):
        for half, source in enumerate((green, hole)):
            pltpu.make_async_copy(
                source.at[:, m, field(a), :],
                gh.at[a, pl.ds(half * MOMENTA + 2 * m, 2)],
                fwd_recv.at[a],
            ).start()

        def one(j, inner):
            peer = lax.rem(m + j, mom)
            for half, source in enumerate((green, hole)):
                pltpu.make_async_remote_copy(
                    src_ref=source.at[:, peer, field(a), :],
                    dst_ref=gh.at[a, pl.ds(half * MOMENTA + 2 * m, 2)],
                    send_sem=fwd_send.at[a],
                    recv_sem=fwd_recv.at[a],
                    device_id={"mom": peer},
                    device_id_type=MESH,
                ).start()
            return inner

        return lax.fori_loop(1, mom, one, carry)

    lax.fori_loop(0, chunks, send_fields, 0)

    lane = lax.broadcasted_iota(jnp.int32, (ORBITALS, 256), 1)
    sub = lax.broadcasted_iota(jnp.int32, (8, 128), 0)
    col = lax.broadcasted_iota(jnp.int32, (8, 128), 1)
    own_orbital = sub == col % ORBITALS
    real_part = col % WIDE < ORBITALS

    def pattern(column):
        return jnp.sum(jnp.where(own_orbital, column, 0.0), axis=0, keepdims=True)

    def swap_parts(v):
        other = jnp.where(real_part, pltpu.roll(v, 128 - ORBITALS, 1), pltpu.roll(v, ORBITALS, 1))
        return jnp.where(real_part, -other, other)

    last = []
    for k in range(2):
        span = decay[k]
        angle = phase[k]
        for j in range(LEVELS):
            reached = lane >= 2**j
            coef[k, j] = jnp.where(reached, jnp.exp(span), 0.0)
            span = span + jnp.where(reached, pltpu.roll(span, 2**j, 1), 0.0)
            angle = angle + jnp.where(reached, pltpu.roll(angle, 2**j, 1), 0.0)
        cosine, sine, growth = jnp.cos(angle), jnp.sin(angle), jnp.exp(span)
        turn[k, 0] = cosine
        turn[k, 1] = sine
        grow[k] = growth
        last.append([pattern(v[:, 255:256]) for v in (cosine, sine, growth)])
    first_k = sub < per_k
    end_cos, end_sin, end_grow = (jnp.where(first_k, u, v) for u, v in zip(*last))
    ends[0] = end_cos
    ends[1] = end_sin
    pst[0] = end_grow * end_cos
    pst[1] = end_grow * end_sin

    def send_product(j, carry):
        pltpu.make_async_remote_copy(
            src_ref=pst, dst_ref=pbox.at[n], send_sem=prod_send, recv_sem=prod_recv,
            device_id={"tm": lax.rem(n + j, tm)}, device_id_type=MESH,
        ).start()
        return carry

    lax.fori_loop(1, tm, send_product, 0)

    def work(a, carry):
        pltpu.make_async_copy(gh.at[a], gh.at[a], fwd_recv.at[a]).wait()
        for h in range(2):
            lanes = slice(128 * h, 128 * h + 128)
            tg[h] = gh[a, 0:MOMENTA, :, lanes].astype(F32).reshape(MOMENTA * WIDE, 128)
            th[h] = gh[a, MOMENTA:, :, lanes].astype(F32).reshape(MOMENTA * WIDE, 128)

        def gather(ref, row):
            parts = [
                jnp.concatenate([ref[h, pl.ds(row + c, MOMENTA, stride=WIDE), :] for h in range(2)], axis=1)
                for c in range(2)
            ]
            return jnp.concatenate(parts, axis=0).astype(BF16)

        for b in range(ORBITALS):
            g = jnp.dot(plus[...], gather(tg, 2 * b), preferred_element_type=F32)
            q = jnp.dot(minus[...], gather(th, 2 * b), preferred_element_type=F32)
            g_re, g_im = g[:MOMENTA], g[MOMENTA:]
            q_re, q_im = q[:MOMENTA], q[MOMENTA:]
            square_re = g_re * g_re - g_im * g_im
            square_im = 2.0 * g_re * g_im
            energy_re = COUPLING * (square_re * q_re - square_im * q_im)
            energy_im = COUPLING * (square_re * q_im + square_im * q_re)
            energy = jnp.concatenate([energy_re, energy_im], axis=0).astype(BF16)
            back = jnp.dot(minus[...], energy, preferred_element_type=F32)
            for h in range(2):
                lanes = slice(128 * h, 128 * h + 128)
                for c in range(2):
                    ts[h, pl.ds(c * ORBITALS + b, MOMENTA, stride=WIDE), :] = back[
                        c * MOMENTA : (c + 1) * MOMENTA, lanes
                    ]
        for h in range(2):
            sb[a, :, :, 128 * h : 128 * h + 128] = ts[h].reshape(MOMENTA, WIDE, 128).astype(BF16)

        pltpu.make_async_copy(sb.at[a, pl.ds(2 * m, 2)], rb.at[a, m], ret_recv.at[a]).start()

        def one(j, inner):
            peer = lax.rem(m + j, mom)
            pltpu.make_async_remote_copy(
                src_ref=sb.at[a, pl.ds(2 * peer, 2)],
                dst_ref=rb.at[a, m],
                send_sem=ret_send.at[a],
                recv_sem=ret_recv.at[a],
                device_id={"mom": peer},
                device_id_type=MESH,
            ).start()
            return inner

        return lax.fori_loop(1, mom, one, carry)

    lax.fori_loop(0, chunks, work, 0)

    def scan_chunk(a):
        slot = a % 2
        pltpu.make_async_copy(rb.at[a], rb.at[a], ret_recv.at[a]).wait()

        def group(i, total):
            k = i // per_k
            t = pl.multiple_of((i % per_k) * ROW_GROUP, ROW_GROUP)
            x = rb[a, pl.ds(t, ROW_GROUP), k].astype(F32)
            x_re, x_im = x[:, :ORBITALS], x[:, ORBITALS:]
            cosine, sine = turn[k, 0], turn[k, 1]
            y_re = cosine * x_re + sine * x_im
            y_im = cosine * x_im - sine * x_re
            for j in range(LEVELS):
                factor = coef[k, j]
                y_re = y_re + factor * pltpu.roll(y_re, 2**j, 2)
                y_im = y_im + factor * pltpu.roll(y_im, 2**j, 2)
            y = jnp.concatenate([y_re, y_im], axis=1)
            local[slot, k, pl.ds(t, ROW_GROUP)] = y
            tail = y.reshape(ROW_GROUP * WIDE, 256)[:, 128:]
            row = jnp.transpose(tail)[127:128, :]
            return jnp.where(sub == i, row, total)

        total = lax.fori_loop(0, groups, group, jnp.zeros((8, 128), F32))
        est[a] = ends[0] * total + ends[1] * swap_parts(total)

        def one(j, carry):
            pltpu.make_async_remote_copy(
                src_ref=est.at[a], dst_ref=ebox.at[a, n], send_sem=end_send.at[a], recv_sem=end_recv.at[a],
                device_id={"tm": lax.rem(n + j, tm)}, device_id_type=MESH,
            ).start()
            return carry

        lax.fori_loop(1, tm, one, 0)

    def finish_chunk(a):
        slot = a % 2
        pltpu.make_async_copy(ebox.at[a, pl.ds(0, tm - 1)], ebox.at[a, pl.ds(0, tm - 1)], end_recv.at[a]).wait()
        enter = jnp.zeros((8, 128), F32)
        for j in range(tm - 1):
            moved = pbox[j, 0] * enter + pbox[j, 1] * swap_parts(enter) + ebox[a, j]
            enter = jnp.where(j < n, moved, enter)
        columns = jnp.transpose(jnp.concatenate([enter, jnp.zeros((120, 128), F32)], axis=0))

        @pl.when(a >= 2)
        def _():
            pltpu.make_async_copy(done.at[slot], out.at[:, :, field(a), :], out_sem.at[slot]).wait()

        for i in range(groups):
            k, t = i // per_k, (i % per_k) * ROW_GROUP
            column = columns[:, i : i + 1].reshape(ROW_GROUP, WIDE, 1)
            r = local[slot, k, t : t + ROW_GROUP]
            growth = grow[k]
            cosine, sine = STEP_WEIGHT * turn[k, 0], STEP_WEIGHT * turn[k, 1]
            r_re = r[:, :ORBITALS] + column[:, :ORBITALS] * growth
            r_im = r[:, ORBITALS:] + column[:, ORBITALS:] * growth
            h_re = (cosine * r_re - sine * r_im).reshape(ROW_GROUP * ORBITALS, 256)
            h_im = (cosine * r_im + sine * r_re).reshape(ROW_GROUP * ORBITALS, 256)
            for h in range(2):
                lanes = slice(128 * h, 128 * h + 128)
                wide[i, h, pl.ds(0, ROW_GROUP * ORBITALS, stride=2), :] = h_re[:, lanes]
                wide[i, h, pl.ds(1, ROW_GROUP * ORBITALS, stride=2), :] = h_im[:, lanes]
                done[slot, k, t : t + ROW_GROUP, :, lanes] = (
                    wide[i, h].reshape(ROW_GROUP, WIDE, 128).astype(BF16)
                )
        pltpu.make_async_copy(done.at[slot], out.at[:, :, field(a), :], out_sem.at[slot]).start()

    pltpu.make_async_copy(pbox.at[pl.ds(0, tm - 1)], pbox.at[pl.ds(0, tm - 1)], prod_recv).wait()

    def history(a, carry):
        scan_chunk(a)

        @pl.when(a >= 1)
        def _():
            finish_chunk(a - 1)

        return carry

    lax.fori_loop(0, chunks, history, 0)
    finish_chunk(jnp.int32(chunks - 1))

    def drain(a, carry):
        pltpu.make_async_copy(gh.at[a, pl.ds(0, 4 * mom - 4)], gh.at[a, pl.ds(0, 4 * mom - 4)], fwd_send.at[a]).wait()
        pltpu.make_async_copy(rb.at[a, pl.ds(0, mom - 1)], rb.at[a, pl.ds(0, mom - 1)], ret_send.at[a]).wait()
        pltpu.make_async_copy(ebox.at[a, pl.ds(0, tm - 1)], ebox.at[a, pl.ds(0, tm - 1)], end_send.at[a]).wait()
        return carry

    lax.fori_loop(0, chunks, drain, 0)
    pltpu.make_async_copy(pbox.at[pl.ds(0, tm - 1)], pbox.at[pl.ds(0, tm - 1)], prod_send).wait()
    for slot in range(2):
        pltpu.make_async_copy(done.at[slot], out.at[:, :, field(0), :], out_sem.at[slot]).wait()


def solution(mesh):
    mom, tm = mesh.shape["mom"], mesh.shape["tm"]

    def shards(green, hole, decay_log, phase_step):
        rows = green.shape[1]
        chunks = ORBITALS
        vmem = pl.BlockSpec(memory_space=pltpu.VMEM)
        anywhere = pl.BlockSpec(memory_space=pl.ANY)
        dma = pltpu.SemaphoreType.DMA
        return pl.pallas_call(
            functools.partial(kernel, mom, tm, rows),
            out_shape=jax.ShapeDtypeStruct(green.shape, BF16),
            in_specs=[anywhere, anywhere, vmem, vmem, vmem, vmem],
            out_specs=anywhere,
            scratch_shapes=[
                pltpu.VMEM((chunks, 2 * MOMENTA, WIDE, 256), BF16),
                pltpu.VMEM((chunks, MOMENTA, WIDE, 256), BF16),
                pltpu.VMEM((chunks, mom, 2, WIDE, 256), BF16),
                pltpu.VMEM((2, MOMENTA * WIDE, 128), F32),
                pltpu.VMEM((2, MOMENTA * WIDE, 128), F32),
                pltpu.VMEM((2, MOMENTA * WIDE, 128), F32),
                pltpu.VMEM((2, LEVELS, ORBITALS, 256), F32),
                pltpu.VMEM((2, 2, ORBITALS, 256), F32),
                pltpu.VMEM((2, ORBITALS, 256), F32),
                pltpu.VMEM((2, 8, 128), F32),
                pltpu.VMEM((2, 2, rows, WIDE, 256), F32),
                pltpu.VMEM((2 * rows // ROW_GROUP, 2, ROW_GROUP * WIDE, 128), F32),
                pltpu.VMEM((2, 2, rows, WIDE, 256), BF16),
                pltpu.VMEM((chunks, 8, 128), F32),
                pltpu.VMEM((chunks, tm, 8, 128), F32),
                pltpu.VMEM((2, 8, 128), F32),
                pltpu.VMEM((tm, 2, 8, 128), F32),
                dma((chunks,)), dma((chunks,)), dma((chunks,)), dma((chunks,)),
                dma((chunks,)), dma((chunks,)), dma(()), dma(()), dma((2,)),
            ],
            compiler_params=pltpu.CompilerParams(
                collective_id=0, has_side_effects=True, vmem_limit_bytes=56 << 20
            ),
        )(green, hole, decay_log, phase_step, transform_table(1.0), transform_table(-1.0))

    in_specs = (
        P("mom", None, None, "tm"),
        P("mom", None, None, "tm"),
        P("mom", None, "tm"),
        P("mom", None, "tm"),
    )
    out_specs = P("mom", None, None, "tm")
    return jax.shard_map(shards, mesh=mesh, in_specs=in_specs, out_specs=out_specs, check_vma=False)
```

```python
import functools
import math

import jax
import jax.numpy as jnp
import numpy as np
from jax import lax
from jax.experimental import pallas as pl
from jax.experimental.pallas import tpu as pltpu
from jax.sharding import PartitionSpec as P

MESH = pl.DeviceIdType.MESH
F32 = jnp.float32
BF16 = jnp.bfloat16
MOMENTA = 64
ORBITALS = 8
WIDE = 2 * ORBITALS
COUPLING = 0.25
STEP_WEIGHT = 0.0625
LEVELS = 8
ROW_GROUP = 8


def transform_table(handed):
    numbers = np.arange(MOMENTA)
    product = (numbers[:, None] * numbers[None, :]) % MOMENTA
    angles = product.astype(np.float32) * np.float32(2.0 * math.pi / MOMENTA)
    scaled = np.float32(1.0 / math.sqrt(MOMENTA))
    cosine = np.cos(angles) * scaled
    sine = np.float32(handed) * np.sin(angles) * scaled
    return jnp.asarray(np.block([[cosine, -sine], [sine, cosine]]).astype(jnp.bfloat16))


def kernel(
    mom, tm, rows,
    green, hole, decay, phase, plus, minus,
    out,
    gh, sb, rb, tg, th, ts, coef, turn, grow, ends, local, wide,
    est, ebox, pst, pbox,
    fwd_send, fwd_recv, ret_send, ret_recv, end_send, end_recv, prod_send, prod_recv,
):
    m = lax.axis_index("mom")
    n = lax.axis_index("tm")
    chunks = ORBITALS
    groups = 2 * rows // ROW_GROUP
    per_k = rows // ROW_GROUP
    side = 8
    across = mom // side
    x, z = m // side, m % side

    def offset(j):
        q, i = j // 8, j % 8
        turned = i // 4
        dz = jnp.where(q == 0, 4 * turned, (4 - q) * (1 - 2 * turned))
        return i % 4, dz

    def target(j):
        dx, dz = offset(j)
        return lax.rem(x + dx, across) * side + lax.rem(z + dz + side, side)

    def origin(j):
        dx, dz = offset(j)
        return lax.rem(x - dx + across, across) * side + lax.rem(z - dz + side, side)

    def field(a):
        return pl.ds(pl.multiple_of(a * WIDE, WIDE), WIDE)

    barrier = pltpu.get_barrier_semaphore()
    ebox[...] = jnp.zeros_like(ebox)
    pbox[...] = jnp.zeros_like(pbox)

    def greet_mom(j, carry):
        pl.semaphore_signal(barrier, inc=1, device_id={"mom": lax.rem(m + j, mom)}, device_id_type=MESH)
        return carry

    def greet_tm(j, carry):
        pl.semaphore_signal(barrier, inc=1, device_id={"tm": lax.rem(n + j, tm)}, device_id_type=MESH)
        return carry

    lax.fori_loop(1, mom, greet_mom, 0)
    lax.fori_loop(1, tm, greet_tm, 0)
    pl.semaphore_wait(barrier, mom + tm - 2)

    def send_fields(a, carry):
        for half, source in enumerate((green, hole)):
            pltpu.make_async_copy(
                source.at[:, m, field(a), :],
                gh.at[a, pl.ds(half * MOMENTA + 2 * m, 2)],
                fwd_recv.at[a],
            ).start()

        def one(j, inner):
            peer = target(j)
            for half, source in enumerate((green, hole)):
                pltpu.make_async_remote_copy(
                    src_ref=source.at[:, peer, field(a), :],
                    dst_ref=gh.at[a, pl.ds(half * MOMENTA + 2 * m, 2)],
                    send_sem=fwd_send.at[a],
                    recv_sem=fwd_recv.at[a],
                    device_id={"mom": peer},
                    device_id_type=MESH,
                ).start()
            return inner

        return lax.fori_loop(1, mom, one, carry)

    lax.fori_loop(0, chunks, send_fields, 0)

    lane = lax.broadcasted_iota(jnp.int32, (ORBITALS, 256), 1)
    sub = lax.broadcasted_iota(jnp.int32, (8, 128), 0)
    col = lax.broadcasted_iota(jnp.int32, (8, 128), 1)
    near = lax.broadcasted_iota(jnp.int32, (ROW_GROUP, ORBITALS, 128), 2)
    own_orbital = sub == col % ORBITALS
    real_part = col % WIDE < ORBITALS

    def pattern(column):
        return jnp.sum(jnp.where(own_orbital, column, 0.0), axis=0, keepdims=True)

    def swap_parts(v):
        other = jnp.where(real_part, pltpu.roll(v, 128 - ORBITALS, 1), pltpu.roll(v, ORBITALS, 1))
        return jnp.where(real_part, -other, other)

    last = []
    for k in range(2):
        span = decay[k]
        angle = phase[k]
        for j in range(LEVELS):
            reached = lane >= 2**j
            coef[k, j] = jnp.where(reached, jnp.exp(span), 0.0)
            span = span + jnp.where(reached, pltpu.roll(span, 2**j, 1), 0.0)
            angle = angle + jnp.where(reached, pltpu.roll(angle, 2**j, 1), 0.0)
        cosine, sine, growth = jnp.cos(angle), jnp.sin(angle), jnp.exp(span)
        turn[k, 0] = cosine
        turn[k, 1] = sine
        grow[k] = growth
        last.append([pattern(v[:, 255:256]) for v in (cosine, sine, growth)])
    first_k = sub < per_k
    end_cos, end_sin, end_grow = (jnp.where(first_k, u, v) for u, v in zip(*last))
    ends[0] = end_cos
    ends[1] = end_sin
    pst[0] = end_grow * end_cos
    pst[1] = end_grow * end_sin

    def send_product(j, carry):
        pltpu.make_async_remote_copy(
            src_ref=pst, dst_ref=pbox.at[n], send_sem=prod_send, recv_sem=prod_recv,
            device_id={"tm": lax.rem(n + j, tm)}, device_id_type=MESH,
        ).start()
        return carry

    lax.fori_loop(1, tm, send_product, 0)

    def work(a, carry):
        pltpu.make_async_copy(gh.at[a], gh.at[a], fwd_recv.at[a]).wait()
        for h in range(2):
            lanes = slice(128 * h, 128 * h + 128)
            tg[h] = gh[a, 0:MOMENTA, :, lanes].astype(F32).reshape(MOMENTA * WIDE, 128)
            th[h] = gh[a, MOMENTA:, :, lanes].astype(F32).reshape(MOMENTA * WIDE, 128)

        def gather(ref, row):
            parts = [
                jnp.concatenate([ref[h, pl.ds(row + c, MOMENTA, stride=WIDE), :] for h in range(2)], axis=1)
                for c in range(2)
            ]
            return jnp.concatenate(parts, axis=0).astype(BF16)

        for b in range(ORBITALS):
            g = jnp.dot(plus[...], gather(tg, 2 * b), preferred_element_type=F32)
            q = jnp.dot(minus[...], gather(th, 2 * b), preferred_element_type=F32)
            g_re, g_im = g[:MOMENTA], g[MOMENTA:]
            q_re, q_im = q[:MOMENTA], q[MOMENTA:]
            square_re = g_re * g_re - g_im * g_im
            square_im = 2.0 * g_re * g_im
            energy_re = COUPLING * (square_re * q_re - square_im * q_im)
            energy_im = COUPLING * (square_re * q_im + square_im * q_re)
            energy = jnp.concatenate([energy_re, energy_im], axis=0).astype(BF16)
            back = jnp.dot(minus[...], energy, preferred_element_type=F32)
            for h in range(2):
                lanes = slice(128 * h, 128 * h + 128)
                for c in range(2):
                    ts[h, pl.ds(c * ORBITALS + b, MOMENTA, stride=WIDE), :] = back[
                        c * MOMENTA : (c + 1) * MOMENTA, lanes
                    ]
        for h in range(2):
            sb[a, :, :, 128 * h : 128 * h + 128] = ts[h].reshape(MOMENTA, WIDE, 128).astype(BF16)

        pltpu.make_async_copy(sb.at[a, pl.ds(2 * m, 2)], rb.at[a, 0], ret_recv.at[a, 0]).start()

        def one(j, inner):
            peer = target(j)
            pltpu.make_async_remote_copy(
                src_ref=sb.at[a, pl.ds(2 * peer, 2)],
                dst_ref=rb.at[a, j],
                send_sem=ret_send.at[a],
                recv_sem=ret_recv.at[a, j // ROW_GROUP],
                device_id={"mom": peer},
                device_id_type=MESH,
            ).start()
            return inner

        return lax.fori_loop(1, mom, one, carry)

    lax.fori_loop(0, chunks, work, 0)

    def scan_chunk(a):
        slot = a % 2

        def group(q, total):
            t = pl.multiple_of(q * ROW_GROUP, ROW_GROUP)
            block = rb.at[a, pl.ds(t, ROW_GROUP)]
            pltpu.make_async_copy(block, block, ret_recv.at[a, q]).wait()
            for k in range(2):
                v = rb[a, pl.ds(t, ROW_GROUP), k].astype(F32)
                cosine, sine = turn[k, 0], turn[k, 1]
                v_re, v_im = v[:, :ORBITALS], v[:, ORBITALS:]
                y_re = cosine * v_re + sine * v_im
                y_im = cosine * v_im - sine * v_re
                parts = []
                for y in (y_re, y_im):
                    lo, hi = y[:, :, :128], y[:, :, 128:]
                    for j in range(LEVELS - 1):
                        factor = coef[k, j]
                        lo_moved, hi_moved = pltpu.roll(lo, 2**j, 2), pltpu.roll(hi, 2**j, 2)
                        hi = hi + factor[:, 128:] * jnp.where(near >= 2**j, hi_moved, lo_moved)
                        lo = lo + factor[:, :128] * lo_moved
                    hi = hi + coef[k, LEVELS - 1][:, 128:] * lo
                    parts.append((lo, hi))
                los = jnp.concatenate([parts[0][0], parts[1][0]], axis=1)
                his = jnp.concatenate([parts[0][1], parts[1][1]], axis=1)
                local[slot, k, pl.ds(t, ROW_GROUP), :, 0:128] = los
                local[slot, k, pl.ds(t, ROW_GROUP), :, 128:256] = his
                row = jnp.transpose(his.reshape(ROW_GROUP * WIDE, 128))[127:128, :]
                total = jnp.where(sub == k * per_k + q, row, total)
            return total

        total = lax.fori_loop(0, per_k, group, jnp.zeros((8, 128), F32))
        est[a] = ends[0] * total + ends[1] * swap_parts(total)

        def one(j, carry):
            pltpu.make_async_remote_copy(
                src_ref=est.at[a], dst_ref=ebox.at[a, n], send_sem=end_send.at[a], recv_sem=end_recv.at[a],
                device_id={"tm": lax.rem(n + j, tm)}, device_id_type=MESH,
            ).start()
            return carry

        lax.fori_loop(1, tm, one, 0)

    def finish_chunk(a):
        slot = a % 2
        pltpu.make_async_copy(ebox.at[a, pl.ds(0, tm - 1)], ebox.at[a, pl.ds(0, tm - 1)], end_recv.at[a]).wait()
        enter = jnp.zeros((8, 128), F32)
        for j in range(tm - 1):
            moved = pbox[j, 0] * enter + pbox[j, 1] * swap_parts(enter) + ebox[a, j]
            enter = jnp.where(j < n, moved, enter)
        columns = jnp.transpose(jnp.concatenate([enter, jnp.zeros((120, 128), F32)], axis=0))

        for i in range(groups):
            k, t = i // per_k, (i % per_k) * ROW_GROUP
            column = columns[:, i : i + 1].reshape(ROW_GROUP, WIDE, 1)
            r = local[slot, k, t : t + ROW_GROUP]
            growth = grow[k]
            cosine, sine = STEP_WEIGHT * turn[k, 0], STEP_WEIGHT * turn[k, 1]
            r_re = r[:, :ORBITALS] + column[:, :ORBITALS] * growth
            r_im = r[:, ORBITALS:] + column[:, ORBITALS:] * growth
            h_re = (cosine * r_re - sine * r_im).reshape(ROW_GROUP * ORBITALS, 256)
            h_im = (cosine * r_im + sine * r_re).reshape(ROW_GROUP * ORBITALS, 256)
            for h in range(2):
                lanes = slice(128 * h, 128 * h + 128)
                wide[i, h, pl.ds(0, ROW_GROUP * ORBITALS, stride=2), :] = h_re[:, lanes]
                wide[i, h, pl.ds(1, ROW_GROUP * ORBITALS, stride=2), :] = h_im[:, lanes]
                whole = wide[i, h].reshape(ROW_GROUP, WIDE, 128).astype(BF16)
                for e in range(ROW_GROUP):
                    out[k, origin(t + e), field(a), lanes] = whole[e]

    pltpu.make_async_copy(pbox.at[pl.ds(0, tm - 1)], pbox.at[pl.ds(0, tm - 1)], prod_recv).wait()

    def history(a, carry):
        scan_chunk(a)

        @pl.when(a >= 1)
        def _():
            finish_chunk(a - 1)

        return carry

    lax.fori_loop(0, chunks, history, 0)
    finish_chunk(jnp.int32(chunks - 1))

    def drain(a, carry):
        pltpu.make_async_copy(gh.at[a, pl.ds(0, 4 * mom - 4)], gh.at[a, pl.ds(0, 4 * mom - 4)], fwd_send.at[a]).wait()
        pltpu.make_async_copy(rb.at[a, pl.ds(0, mom - 1)], rb.at[a, pl.ds(0, mom - 1)], ret_send.at[a]).wait()
        pltpu.make_async_copy(ebox.at[a, pl.ds(0, tm - 1)], ebox.at[a, pl.ds(0, tm - 1)], end_send.at[a]).wait()
        return carry

    lax.fori_loop(0, chunks, drain, 0)
    pltpu.make_async_copy(pbox.at[pl.ds(0, tm - 1)], pbox.at[pl.ds(0, tm - 1)], prod_send).wait()


def solution(mesh):
    mom, tm = mesh.shape["mom"], mesh.shape["tm"]

    def shards(green, hole, decay_log, phase_step):
        rows = green.shape[1]
        chunks = ORBITALS
        vmem = pl.BlockSpec(memory_space=pltpu.VMEM)
        anywhere = pl.BlockSpec(memory_space=pl.ANY)
        dma = pltpu.SemaphoreType.DMA
        return pl.pallas_call(
            functools.partial(kernel, mom, tm, rows),
            out_shape=pltpu.VMEM(green.shape, BF16),
            in_specs=[anywhere, anywhere, vmem, vmem, vmem, vmem],
            out_specs=vmem,
            scratch_shapes=[
                pltpu.VMEM((chunks, 2 * MOMENTA, WIDE, 256), BF16),
                pltpu.VMEM((chunks, MOMENTA, WIDE, 256), BF16),
                pltpu.VMEM((chunks, mom, 2, WIDE, 256), BF16),
                pltpu.VMEM((2, MOMENTA * WIDE, 128), F32),
                pltpu.VMEM((2, MOMENTA * WIDE, 128), F32),
                pltpu.VMEM((2, MOMENTA * WIDE, 128), F32),
                pltpu.VMEM((2, LEVELS, ORBITALS, 256), F32),
                pltpu.VMEM((2, 2, ORBITALS, 256), F32),
                pltpu.VMEM((2, ORBITALS, 256), F32),
                pltpu.VMEM((2, 8, 128), F32),
                pltpu.VMEM((2, 2, rows, WIDE, 256), F32),
                pltpu.VMEM((2 * rows // ROW_GROUP, 2, ROW_GROUP * WIDE, 128), F32),
                pltpu.VMEM((chunks, 8, 128), F32),
                pltpu.VMEM((chunks, tm, 8, 128), F32),
                pltpu.VMEM((2, 8, 128), F32),
                pltpu.VMEM((tm, 2, 8, 128), F32),
                dma((chunks,)), dma((chunks,)), dma((chunks,)), dma((chunks, rows // ROW_GROUP)),
                dma((chunks,)), dma((chunks,)), dma(()), dma(()),
            ],
            compiler_params=pltpu.CompilerParams(
                collective_id=0, has_side_effects=True, vmem_limit_bytes=56 << 20
            ),
        )(green, hole, decay_log, phase_step, transform_table(1.0), transform_table(-1.0))

    in_specs = (
        P("mom", None, None, "tm"),
        P("mom", None, None, "tm"),
        P("mom", None, "tm"),
        P("mom", None, "tm"),
    )
    out_specs = P("mom", None, None, "tm")
    return jax.shard_map(shards, mesh=mesh, in_specs=in_specs, out_specs=out_specs, check_vma=False)
```

```python
import functools
import math

import jax
import jax.numpy as jnp
import numpy as np
from jax import lax
from jax.experimental import pallas as pl
from jax.experimental.pallas import tpu as pltpu
from jax.sharding import PartitionSpec as P

MESH = pl.DeviceIdType.MESH
F32 = jnp.float32
BF16 = jnp.bfloat16
MOMENTA = 64
ORBITALS = 8
WIDE = 2 * ORBITALS
COUPLING = 0.25
STEP_WEIGHT = 0.0625
LEVELS = 8
ROW_GROUP = 8


def transform_table(handed):
    numbers = np.arange(MOMENTA)
    product = (numbers[:, None] * numbers[None, :]) % MOMENTA
    angles = product.astype(np.float32) * np.float32(2.0 * math.pi / MOMENTA)
    scaled = np.float32(1.0 / math.sqrt(MOMENTA))
    cosine = np.cos(angles) * scaled
    sine = np.float32(handed) * np.sin(angles) * scaled
    return jnp.asarray(np.block([[cosine, -sine], [sine, cosine]]).astype(jnp.bfloat16))


def kernel(
    mom, tm, rows,
    green, hole, decay, phase, plus, minus,
    out,
    gh, sb, rb, tg, th, ts, coef, turn, grow, heavy, reach, local, wide,
    est, ebox, pst, pbox,
    fwd_send, fwd_recv, ret_send, ret_recv, end_send, end_recv, prod_send, prod_recv, line_z, line_x,
):
    m = lax.axis_index("mom")
    n = lax.axis_index("tm")
    chunks = ORBITALS
    groups = 2 * rows // ROW_GROUP
    per_k = rows // ROW_GROUP
    side = 8
    across = mom // side
    x, z = m // side, m % side

    def offset(j):
        q, i = j // 8, j % 8
        turned = i // 4
        dz = jnp.where(q == 0, 4 * turned, (4 - q) * (1 - 2 * turned))
        return i % 4, dz

    def target(j):
        dx, dz = offset(j)
        return lax.rem(x + dx, across) * side + lax.rem(z + dz + side, side)

    def origin(j):
        dx, dz = offset(j)
        return lax.rem(x - dx + across, across) * side + lax.rem(z - dz + side, side)

    def field(a):
        return pl.ds(pl.multiple_of(a * WIDE, WIDE), WIDE)

    barrier = pltpu.get_barrier_semaphore()
    ebox[...] = jnp.zeros_like(ebox)
    pbox[...] = jnp.zeros_like(pbox)

    def at(dx, dz):
        return lax.rem(x + dx + across, across) * side + lax.rem(z + dz + side, side)

    def greet(semaphore, **where):
        pl.semaphore_signal(semaphore, inc=1, device_id=where, device_id_type=MESH)

    for dz in (1, -1, 2, -2):
        greet(barrier, mom=at(0, dz))
    for dx in range(1, across):
        greet(barrier, mom=at(dx, 0))

    def greet_tm(j, carry):
        greet(barrier, tm=lax.rem(n + j, tm))
        return carry

    lax.fori_loop(1, tm, greet_tm, 0)
    pl.semaphore_wait(barrier, 4 + across - 1 + tm - 1)
    for dz in (2, -2):
        greet(line_z, mom=at(0, dz))

    def send_field(a, j):
        peer = target(j)
        for half, source in enumerate((green, hole)):
            pltpu.make_async_remote_copy(
                src_ref=source.at[:, peer, field(a), :],
                dst_ref=gh.at[a, pl.ds(half * MOMENTA + 2 * m, 2)],
                send_sem=fwd_send.at[a],
                recv_sem=fwd_recv.at[a],
                device_id={"mom": peer},
                device_id_type=MESH,
            ).start()

    def send_near(a, carry):
        for j in (16, 20, 24, 28):
            send_field(a, j)
        return carry

    def send_far(a, carry):
        for half, source in enumerate((green, hole)):
            pltpu.make_async_copy(
                source.at[:, m, field(a), :],
                gh.at[a, pl.ds(half * MOMENTA + 2 * m, 2)],
                fwd_recv.at[a],
            ).start()

        def one(j, inner):
            @pl.when(jnp.logical_or(j < 16, j % 4 != 0))
            def _():
                send_field(a, j)

            return inner

        return lax.fori_loop(1, mom, one, carry)

    lax.fori_loop(0, chunks, send_near, 0)
    pl.semaphore_wait(line_z, 2)
    for dx in range(1, across):
        greet(line_x, mom=at(dx, 0))
    pl.semaphore_wait(line_x, across - 1)
    lax.fori_loop(0, chunks, send_far, 0)

    lane = lax.broadcasted_iota(jnp.int32, (ORBITALS, 256), 1)
    sub = lax.broadcasted_iota(jnp.int32, (8, 128), 0)
    col = lax.broadcasted_iota(jnp.int32, (8, 128), 1)
    near = lax.broadcasted_iota(jnp.int32, (ROW_GROUP, ORBITALS, 128), 2)
    own_orbital = sub == col % ORBITALS
    real_part = col % WIDE < ORBITALS

    def pattern(column):
        return jnp.sum(jnp.where(own_orbital, column, 0.0), axis=0, keepdims=True)

    def swap_parts(v):
        other = jnp.where(real_part, pltpu.roll(v, 128 - ORBITALS, 1), pltpu.roll(v, ORBITALS, 1))
        return jnp.where(real_part, -other, other)

    last = []
    for k in range(2):
        span = decay[k]
        angle = phase[k]
        for j in range(LEVELS):
            reached = lane >= 2**j
            coef[k, j] = jnp.where(reached, jnp.exp(span), 0.0)
            span = span + jnp.where(reached, pltpu.roll(span, 2**j, 1), 0.0)
            angle = angle + jnp.where(reached, pltpu.roll(angle, 2**j, 1), 0.0)
        cosine, sine, growth = jnp.cos(angle), jnp.sin(angle), jnp.exp(span)
        rest = jnp.where(lane < 255, pltpu.roll(decay[k], 255, 1), 0.0)
        for j in range(LEVELS):
            rest = rest + jnp.where(lane < 256 - 2**j, pltpu.roll(rest, 256 - 2**j, 1), 0.0)
        fade = jnp.exp(rest)
        to_turn = angle[:, 255:256] - angle
        weight = jnp.concatenate([fade * jnp.cos(to_turn), fade * jnp.sin(to_turn)], axis=0)
        high = weight.astype(BF16)
        heavy[k] = jnp.concatenate([high, (weight - high.astype(F32)).astype(BF16)], axis=0)
        turn[k, 0] = cosine
        turn[k, 1] = sine
        grow[k] = growth
        last.append([pattern(v[:, 255:256]) for v in (cosine, sine, growth)])
    first_k = sub < per_k
    end_cos, end_sin, end_grow = (jnp.where(first_k, u, v) for u, v in zip(*last))
    pst[0] = end_grow * end_cos
    pst[1] = end_grow * end_sin

    def send_product(j, carry):
        pltpu.make_async_remote_copy(
            src_ref=pst, dst_ref=pbox.at[n], send_sem=prod_send, recv_sem=prod_recv,
            device_id={"tm": lax.rem(n + j, tm)}, device_id_type=MESH,
        ).start()
        return carry

    lax.fori_loop(1, tm, send_product, 0)

    def work(a, carry):
        pltpu.make_async_copy(gh.at[a], gh.at[a], fwd_recv.at[a]).wait()
        for h in range(2):
            lanes = slice(128 * h, 128 * h + 128)
            tg[h] = gh[a, 0:MOMENTA, :, lanes].astype(F32).reshape(MOMENTA * WIDE, 128)
            th[h] = gh[a, MOMENTA:, :, lanes].astype(F32).reshape(MOMENTA * WIDE, 128)

        def gather(ref, row):
            parts = [
                jnp.concatenate([ref[h, pl.ds(row + c, MOMENTA, stride=WIDE), :] for h in range(2)], axis=1)
                for c in range(2)
            ]
            return jnp.concatenate(parts, axis=0).astype(BF16)

        for b in range(ORBITALS):
            g = jnp.dot(plus[...], gather(tg, 2 * b), preferred_element_type=F32)
            q = jnp.dot(minus[...], gather(th, 2 * b), preferred_element_type=F32)
            g_re, g_im = g[:MOMENTA], g[MOMENTA:]
            q_re, q_im = q[:MOMENTA], q[MOMENTA:]
            square_re = g_re * g_re - g_im * g_im
            square_im = 2.0 * g_re * g_im
            energy_re = COUPLING * (square_re * q_re - square_im * q_im)
            energy_im = COUPLING * (square_re * q_im + square_im * q_re)
            energy = jnp.concatenate([energy_re, energy_im], axis=0).astype(BF16)
            back = jnp.dot(minus[...], energy, preferred_element_type=F32)
            for h in range(2):
                lanes = slice(128 * h, 128 * h + 128)
                for c in range(2):
                    ts[h, pl.ds(c * ORBITALS + b, MOMENTA, stride=WIDE), :] = back[
                        c * MOMENTA : (c + 1) * MOMENTA, lanes
                    ]
        for h in range(2):
            sb[a, :, :, 128 * h : 128 * h + 128] = ts[h].reshape(MOMENTA, WIDE, 128).astype(BF16)

        pltpu.make_async_copy(sb.at[a, pl.ds(2 * m, 2)], rb.at[a, 0], ret_recv.at[a, 0]).start()

        def one(j, inner):
            peer = target(j)
            pltpu.make_async_remote_copy(
                src_ref=sb.at[a, pl.ds(2 * peer, 2)],
                dst_ref=rb.at[a, j],
                send_sem=ret_send.at[a],
                recv_sem=ret_recv.at[a, j // ROW_GROUP],
                device_id={"mom": peer},
                device_id_type=MESH,
            ).start()
            return inner

        return lax.fori_loop(1, mom, one, carry)

    lax.fori_loop(0, chunks, work, 0)

    def scan_chunk(a):
        slot = a % 2

        def ending(q, total):
            t = pl.multiple_of(q * ROW_GROUP, ROW_GROUP)
            block = rb.at[a, pl.ds(t, ROW_GROUP)]
            pltpu.make_async_copy(block, block, ret_recv.at[a, q]).wait()
            for k in range(2):
                v = rb[a, pl.ds(t, ROW_GROUP), k].reshape(ROW_GROUP * WIDE, 256)
                r = lax.dot_general(heavy[k], v, (((1,), (1,)), ((), ())), preferred_element_type=F32)
                r = r[:WIDE] + r[WIDE:]
                p = jnp.sum(jnp.where(own_orbital, r[:ORBITALS], 0.0), axis=0, keepdims=True)
                w = jnp.sum(jnp.where(own_orbital, r[ORBITALS:], 0.0), axis=0, keepdims=True)
                row = p + swap_parts(jnp.broadcast_to(w, (8, 128)))
                total = jnp.where(sub == k * per_k + q, row, total)
            return total

        est[a] = lax.fori_loop(0, per_k, ending, jnp.zeros((8, 128), F32))

        def one(j, carry):
            pltpu.make_async_remote_copy(
                src_ref=est.at[a], dst_ref=ebox.at[a, n], send_sem=end_send.at[a], recv_sem=end_recv.at[a],
                device_id={"tm": lax.rem(n + j, tm)}, device_id_type=MESH,
            ).start()
            return carry

        lax.fori_loop(1, tm, one, 0)

        def group(q, carry):
            t = pl.multiple_of(q * ROW_GROUP, ROW_GROUP)
            for k in range(2):
                v = rb[a, pl.ds(t, ROW_GROUP), k].astype(F32)
                cosine, sine = turn[k, 0], turn[k, 1]
                v_re, v_im = v[:, :ORBITALS], v[:, ORBITALS:]
                y_re = cosine * v_re + sine * v_im
                y_im = cosine * v_im - sine * v_re
                parts = []
                for y in (y_re, y_im):
                    lo, hi = y[:, :, :128], y[:, :, 128:]
                    for j in range(LEVELS - 1):
                        factor = coef[k, j]
                        lo_moved, hi_moved = pltpu.roll(lo, 2**j, 2), pltpu.roll(hi, 2**j, 2)
                        hi = hi + factor[:, 128:] * jnp.where(near >= 2**j, hi_moved, lo_moved)
                        lo = lo + factor[:, :128] * lo_moved
                    hi = hi + coef[k, LEVELS - 1][:, 128:] * lo
                    parts.append((lo, hi))
                los = jnp.concatenate([parts[0][0], parts[1][0]], axis=1)
                his = jnp.concatenate([parts[0][1], parts[1][1]], axis=1)
                local[slot, k, pl.ds(t, ROW_GROUP), :, 0:128] = los
                local[slot, k, pl.ds(t, ROW_GROUP), :, 128:256] = his
            return carry

        lax.fori_loop(0, per_k, group, 0)

    def finish_chunk(a):
        slot = a % 2
        pltpu.make_async_copy(ebox.at[a, pl.ds(0, tm - 1)], ebox.at[a, pl.ds(0, tm - 1)], end_recv.at[a]).wait()
        enter = jnp.zeros((8, 128), F32)
        for j in range(tm - 1):
            enter = enter + (reach[j, 0] * ebox[a, j] + reach[j, 1] * swap_parts(ebox[a, j]))
        columns = jnp.transpose(jnp.concatenate([enter, jnp.zeros((120, 128), F32)], axis=0))

        for i in range(groups):
            k, t = i // per_k, (i % per_k) * ROW_GROUP
            column = columns[:, i : i + 1].reshape(ROW_GROUP, WIDE, 1)
            r = local[slot, k, t : t + ROW_GROUP]
            growth = grow[k]
            cosine, sine = STEP_WEIGHT * turn[k, 0], STEP_WEIGHT * turn[k, 1]
            r_re = r[:, :ORBITALS] + column[:, :ORBITALS] * growth
            r_im = r[:, ORBITALS:] + column[:, ORBITALS:] * growth
            h_re = (cosine * r_re - sine * r_im).reshape(ROW_GROUP * ORBITALS, 256)
            h_im = (cosine * r_im + sine * r_re).reshape(ROW_GROUP * ORBITALS, 256)
            for h in range(2):
                lanes = slice(128 * h, 128 * h + 128)
                wide[i, h, pl.ds(0, ROW_GROUP * ORBITALS, stride=2), :] = h_re[:, lanes]
                wide[i, h, pl.ds(1, ROW_GROUP * ORBITALS, stride=2), :] = h_im[:, lanes]
                whole = wide[i, h].reshape(ROW_GROUP, WIDE, 128).astype(BF16)
                for e in range(ROW_GROUP):
                    out[k, origin(t + e), field(a), lanes] = whole[e]

    pltpu.make_async_copy(pbox.at[pl.ds(0, tm - 1)], pbox.at[pl.ds(0, tm - 1)], prod_recv).wait()
    through_re, through_im = jnp.ones((8, 128), F32), jnp.zeros((8, 128), F32)
    for j in range(tm - 2, -1, -1):
        p_re, p_im = pbox[j, 0], pbox[j, 1]
        earlier = j < n
        reach[j, 0] = jnp.where(earlier, through_re, 0.0)
        reach[j, 1] = jnp.where(earlier, through_im, 0.0)
        through_re, through_im = (
            jnp.where(earlier, through_re * p_re - through_im * p_im, through_re),
            jnp.where(earlier, through_re * p_im + through_im * p_re, through_im),
        )

    def history(a, carry):
        scan_chunk(a)

        @pl.when(a >= 1)
        def _():
            finish_chunk(a - 1)

        return carry

    lax.fori_loop(0, chunks, history, 0)
    finish_chunk(jnp.int32(chunks - 1))

    def drain(a, carry):
        pltpu.make_async_copy(gh.at[a, pl.ds(0, 4 * mom - 4)], gh.at[a, pl.ds(0, 4 * mom - 4)], fwd_send.at[a]).wait()
        pltpu.make_async_copy(rb.at[a, pl.ds(0, mom - 1)], rb.at[a, pl.ds(0, mom - 1)], ret_send.at[a]).wait()
        pltpu.make_async_copy(ebox.at[a, pl.ds(0, tm - 1)], ebox.at[a, pl.ds(0, tm - 1)], end_send.at[a]).wait()
        return carry

    lax.fori_loop(0, chunks, drain, 0)
    pltpu.make_async_copy(pbox.at[pl.ds(0, tm - 1)], pbox.at[pl.ds(0, tm - 1)], prod_send).wait()


def solution(mesh):
    mom, tm = mesh.shape["mom"], mesh.shape["tm"]

    def shards(green, hole, decay_log, phase_step):
        rows = green.shape[1]
        chunks = ORBITALS
        vmem = pl.BlockSpec(memory_space=pltpu.VMEM)
        anywhere = pl.BlockSpec(memory_space=pl.ANY)
        dma = pltpu.SemaphoreType.DMA
        return pl.pallas_call(
            functools.partial(kernel, mom, tm, rows),
            out_shape=pltpu.VMEM(green.shape, BF16),
            in_specs=[anywhere, anywhere, vmem, vmem, vmem, vmem],
            out_specs=vmem,
            scratch_shapes=[
                pltpu.VMEM((chunks, 2 * MOMENTA, WIDE, 256), BF16),
                pltpu.VMEM((chunks, MOMENTA, WIDE, 256), BF16),
                pltpu.VMEM((chunks, mom, 2, WIDE, 256), BF16),
                pltpu.VMEM((2, MOMENTA * WIDE, 128), F32),
                pltpu.VMEM((2, MOMENTA * WIDE, 128), F32),
                pltpu.VMEM((2, MOMENTA * WIDE, 128), F32),
                pltpu.VMEM((2, LEVELS, ORBITALS, 256), F32),
                pltpu.VMEM((2, 2, ORBITALS, 256), F32),
                pltpu.VMEM((2, ORBITALS, 256), F32),
                pltpu.VMEM((2, 2 * WIDE, 256), BF16),
                pltpu.VMEM((tm - 1, 2, 8, 128), F32),
                pltpu.VMEM((2, 2, rows, WIDE, 256), F32),
                pltpu.VMEM((2 * rows // ROW_GROUP, 2, ROW_GROUP * WIDE, 128), F32),
                pltpu.VMEM((chunks, 8, 128), F32),
                pltpu.VMEM((chunks, tm, 8, 128), F32),
                pltpu.VMEM((2, 8, 128), F32),
                pltpu.VMEM((tm, 2, 8, 128), F32),
                dma((chunks,)), dma((chunks,)), dma((chunks,)), dma((chunks, rows // ROW_GROUP)),
                dma((chunks,)), dma((chunks,)), dma(()), dma(()), pltpu.SemaphoreType.REGULAR, pltpu.SemaphoreType.REGULAR,
            ],
            compiler_params=pltpu.CompilerParams(
                collective_id=0, has_side_effects=True, vmem_limit_bytes=56 << 20
            ),
        )(green, hole, decay_log, phase_step, transform_table(1.0), transform_table(-1.0))

    in_specs = (
        P("mom", None, None, "tm"),
        P("mom", None, None, "tm"),
        P("mom", None, "tm"),
        P("mom", None, "tm"),
    )
    out_specs = P("mom", None, None, "tm")
    return jax.shard_map(shards, mesh=mesh, in_specs=in_specs, out_specs=out_specs, check_vma=False)
```

```python
import functools
import math

import jax
import jax.numpy as jnp
import numpy as np
from jax import lax
from jax.experimental import pallas as pl
from jax.experimental.pallas import tpu as pltpu
from jax.sharding import PartitionSpec as P

MESH = pl.DeviceIdType.MESH
F32 = jnp.float32
BF16 = jnp.bfloat16
MOMENTA = 64
ORBITALS = 8
WIDE = 2 * ORBITALS
COUPLING = 0.25
STEP_WEIGHT = 0.0625
LEVELS = 8
ROW_GROUP = 8


def transform_table(handed):
    numbers = np.arange(MOMENTA)
    product = (numbers[:, None] * numbers[None, :]) % MOMENTA
    angles = product.astype(np.float32) * np.float32(2.0 * math.pi / MOMENTA)
    scaled = np.float32(1.0 / math.sqrt(MOMENTA))
    cosine = np.cos(angles) * scaled
    sine = np.float32(handed) * np.sin(angles) * scaled
    return jnp.asarray(np.block([[cosine, -sine], [sine, cosine]]).astype(jnp.bfloat16))


def kernel(
    mom, tm, rows,
    green, hole, decay_in, phase_in, plus_in, minus_in,
    out,
    decay, phase, plus, minus, gh, sb, rb, tg, th, ts, coef, turn, grow, heavy, reach, local, wide,
    est, ebox, pst, pbox,
    fwd_send, fwd_recv, ret_send, ret_recv, end_send, end_recv, prod_send, prod_recv, table_sem, line_z, line_x,
):
    m = lax.axis_index("mom")
    n = lax.axis_index("tm")
    chunks = ORBITALS
    groups = 2 * rows // ROW_GROUP
    per_k = rows // ROW_GROUP
    side = 8
    across = mom // side
    x, z = m // side, m % side

    def offset(j):
        q, i = j // 8, j % 8
        turned = i // 4
        dz = jnp.where(q == 0, 4 * turned, (4 - q) * (1 - 2 * turned))
        return i % 4, dz

    def target(j):
        dx, dz = offset(j)
        return lax.rem(x + dx, across) * side + lax.rem(z + dz + side, side)

    def origin(j):
        dx, dz = offset(j)
        return lax.rem(x - dx + across, across) * side + lax.rem(z - dz + side, side)

    def field(a):
        return pl.ds(pl.multiple_of(a * WIDE, WIDE), WIDE)

    barrier = pltpu.get_barrier_semaphore()
    ebox[...] = jnp.zeros_like(ebox)
    pbox[...] = jnp.zeros_like(pbox)

    def at(dx, dz):
        return lax.rem(x + dx + across, across) * side + lax.rem(z + dz + side, side)

    def greet(semaphore, **where):
        pl.semaphore_signal(semaphore, inc=1, device_id=where, device_id_type=MESH)

    for dz in (1, -1, 2, -2):
        greet(barrier, mom=at(0, dz))
    for dx in range(1, across):
        greet(barrier, mom=at(dx, 0))

    def greet_tm(j, carry):
        greet(barrier, tm=lax.rem(n + j, tm))
        return carry

    lax.fori_loop(1, tm, greet_tm, 0)
    tables = [
        pltpu.make_async_copy(source, kept, table_sem.at[i])
        for i, (source, kept) in enumerate(
            ((decay_in, decay), (phase_in, phase), (plus_in, plus), (minus_in, minus))
        )
    ]
    for copy in tables:
        copy.start()
    pl.semaphore_wait(barrier, 4 + across - 1 + tm - 1)
    for dz in (2, -2):
        greet(line_z, mom=at(0, dz))

    def send_field(a, j):
        peer = target(j)
        for half, source in enumerate((green, hole)):
            pltpu.make_async_remote_copy(
                src_ref=source.at[:, peer, field(a), :],
                dst_ref=gh.at[a, pl.ds(half * MOMENTA + 2 * m, 2)],
                send_sem=fwd_send.at[a],
                recv_sem=fwd_recv.at[a],
                device_id={"mom": peer},
                device_id_type=MESH,
            ).start()

    def send_near(a, carry):
        for j in (16, 20, 24, 28):
            send_field(a, j)
        return carry

    def send_far(a, carry):
        for half, source in enumerate((green, hole)):
            pltpu.make_async_copy(
                source.at[:, m, field(a), :],
                gh.at[a, pl.ds(half * MOMENTA + 2 * m, 2)],
                fwd_recv.at[a],
            ).start()

        def one(j, inner):
            @pl.when(jnp.logical_or(j < 16, j % 4 != 0))
            def _():
                send_field(a, j)

            return inner

        return lax.fori_loop(1, mom, one, carry)

    lax.fori_loop(0, chunks, send_near, 0)
    pl.semaphore_wait(line_z, 2)
    for dx in range(1, across):
        greet(line_x, mom=at(dx, 0))
    pl.semaphore_wait(line_x, across - 1)
    lax.fori_loop(0, chunks, send_far, 0)

    for copy in tables:
        copy.wait()
    lane = lax.broadcasted_iota(jnp.int32, (ORBITALS, 256), 1)
    sub = lax.broadcasted_iota(jnp.int32, (8, 128), 0)
    col = lax.broadcasted_iota(jnp.int32, (8, 128), 1)
    near = lax.broadcasted_iota(jnp.int32, (ROW_GROUP, ORBITALS, 128), 2)
    own_orbital = sub == col % ORBITALS
    real_part = col % WIDE < ORBITALS

    def pattern(column):
        return jnp.sum(jnp.where(own_orbital, column, 0.0), axis=0, keepdims=True)

    def swap_parts(v):
        other = jnp.where(real_part, pltpu.roll(v, 128 - ORBITALS, 1), pltpu.roll(v, ORBITALS, 1))
        return jnp.where(real_part, -other, other)

    last = []
    for k in range(2):
        span = decay[k]
        angle = phase[k]
        for j in range(LEVELS):
            reached = lane >= 2**j
            coef[k, j] = jnp.where(reached, jnp.exp(span), 0.0)
            span = span + jnp.where(reached, pltpu.roll(span, 2**j, 1), 0.0)
            angle = angle + jnp.where(reached, pltpu.roll(angle, 2**j, 1), 0.0)
        cosine, sine, growth = jnp.cos(angle), jnp.sin(angle), jnp.exp(span)
        rest = jnp.where(lane < 255, pltpu.roll(decay[k], 255, 1), 0.0)
        for j in range(LEVELS):
            rest = rest + jnp.where(lane < 256 - 2**j, pltpu.roll(rest, 256 - 2**j, 1), 0.0)
        fade = jnp.exp(rest)
        to_turn = angle[:, 255:256] - angle
        weight = jnp.concatenate([fade * jnp.cos(to_turn), fade * jnp.sin(to_turn)], axis=0)
        high = weight.astype(BF16)
        heavy[k] = jnp.concatenate([high, (weight - high.astype(F32)).astype(BF16)], axis=0)
        turn[k, 0] = cosine
        turn[k, 1] = sine
        grow[k] = growth
        last.append([pattern(v[:, 255:256]) for v in (cosine, sine, growth)])
    first_k = sub < per_k
    end_cos, end_sin, end_grow = (jnp.where(first_k, u, v) for u, v in zip(*last))
    pst[0] = end_grow * end_cos
    pst[1] = end_grow * end_sin

    def send_product(j, carry):
        pltpu.make_async_remote_copy(
            src_ref=pst, dst_ref=pbox.at[n], send_sem=prod_send, recv_sem=prod_recv,
            device_id={"tm": lax.rem(n + j, tm)}, device_id_type=MESH,
        ).start()
        return carry

    lax.fori_loop(1, tm, send_product, 0)

    def work(a, carry):
        pltpu.make_async_copy(gh.at[a], gh.at[a], fwd_recv.at[a]).wait()
        for h in range(2):
            lanes = slice(128 * h, 128 * h + 128)
            tg[h] = gh[a, 0:MOMENTA, :, lanes].astype(F32).reshape(MOMENTA * WIDE, 128)
            th[h] = gh[a, MOMENTA:, :, lanes].astype(F32).reshape(MOMENTA * WIDE, 128)

        def gather(ref, row):
            parts = [
                jnp.concatenate([ref[h, pl.ds(row + c, MOMENTA, stride=WIDE), :] for h in range(2)], axis=1)
                for c in range(2)
            ]
            return jnp.concatenate(parts, axis=0).astype(BF16)

        for b in range(ORBITALS):
            g = jnp.dot(plus[...], gather(tg, 2 * b), preferred_element_type=F32)
            q = jnp.dot(minus[...], gather(th, 2 * b), preferred_element_type=F32)
            g_re, g_im = g[:MOMENTA], g[MOMENTA:]
            q_re, q_im = q[:MOMENTA], q[MOMENTA:]
            square_re = g_re * g_re - g_im * g_im
            square_im = 2.0 * g_re * g_im
            energy_re = COUPLING * (square_re * q_re - square_im * q_im)
            energy_im = COUPLING * (square_re * q_im + square_im * q_re)
            energy = jnp.concatenate([energy_re, energy_im], axis=0).astype(BF16)
            back = jnp.dot(minus[...], energy, preferred_element_type=F32)
            for h in range(2):
                lanes = slice(128 * h, 128 * h + 128)
                for c in range(2):
                    ts[h, pl.ds(c * ORBITALS + b, MOMENTA, stride=WIDE), :] = back[
                        c * MOMENTA : (c + 1) * MOMENTA, lanes
                    ]
        for h in range(2):
            sb[a, :, :, 128 * h : 128 * h + 128] = ts[h].reshape(MOMENTA, WIDE, 128).astype(BF16)

        pltpu.make_async_copy(sb.at[a, pl.ds(2 * m, 2)], rb.at[a, 0], ret_recv.at[a, 0]).start()

        def one(j, inner):
            peer = target(j)
            pltpu.make_async_remote_copy(
                src_ref=sb.at[a, pl.ds(2 * peer, 2)],
                dst_ref=rb.at[a, j],
                send_sem=ret_send.at[a],
                recv_sem=ret_recv.at[a, j // ROW_GROUP],
                device_id={"mom": peer},
                device_id_type=MESH,
            ).start()
            return inner

        return lax.fori_loop(1, mom, one, carry)

    lax.fori_loop(0, chunks, work, 0)

    def scan_chunk(a):
        slot = a % 2

        def ending(q, total):
            t = pl.multiple_of(q * ROW_GROUP, ROW_GROUP)
            block = rb.at[a, pl.ds(t, ROW_GROUP)]
            pltpu.make_async_copy(block, block, ret_recv.at[a, q]).wait()
            for k in range(2):
                v = rb[a, pl.ds(t, ROW_GROUP), k].reshape(ROW_GROUP * WIDE, 256)
                r = lax.dot_general(heavy[k], v, (((1,), (1,)), ((), ())), preferred_element_type=F32)
                r = r[:WIDE] + r[WIDE:]
                p = jnp.sum(jnp.where(own_orbital, r[:ORBITALS], 0.0), axis=0, keepdims=True)
                w = jnp.sum(jnp.where(own_orbital, r[ORBITALS:], 0.0), axis=0, keepdims=True)
                row = p + swap_parts(jnp.broadcast_to(w, (8, 128)))
                total = jnp.where(sub == k * per_k + q, row, total)
            return total

        est[a] = lax.fori_loop(0, per_k, ending, jnp.zeros((8, 128), F32))

        def one(j, carry):
            pltpu.make_async_remote_copy(
                src_ref=est.at[a], dst_ref=ebox.at[a, n], send_sem=end_send.at[a], recv_sem=end_recv.at[a],
                device_id={"tm": lax.rem(n + j, tm)}, device_id_type=MESH,
            ).start()
            return carry

        lax.fori_loop(1, tm, one, 0)

        def group(q, carry):
            t = pl.multiple_of(q * ROW_GROUP, ROW_GROUP)
            for k in range(2):
                v = rb[a, pl.ds(t, ROW_GROUP), k].astype(F32)
                cosine, sine = turn[k, 0], turn[k, 1]
                v_re, v_im = v[:, :ORBITALS], v[:, ORBITALS:]
                y_re = cosine * v_re + sine * v_im
                y_im = cosine * v_im - sine * v_re
                parts = []
                for y in (y_re, y_im):
                    lo, hi = y[:, :, :128], y[:, :, 128:]
                    for j in range(LEVELS - 1):
                        factor = coef[k, j]
                        lo_moved, hi_moved = pltpu.roll(lo, 2**j, 2), pltpu.roll(hi, 2**j, 2)
                        hi = hi + factor[:, 128:] * jnp.where(near >= 2**j, hi_moved, lo_moved)
                        lo = lo + factor[:, :128] * lo_moved
                    hi = hi + coef[k, LEVELS - 1][:, 128:] * lo
                    parts.append((lo, hi))
                los = jnp.concatenate([parts[0][0], parts[1][0]], axis=1)
                his = jnp.concatenate([parts[0][1], parts[1][1]], axis=1)
                local[slot, k, pl.ds(t, ROW_GROUP), :, 0:128] = los
                local[slot, k, pl.ds(t, ROW_GROUP), :, 128:256] = his
            return carry

        lax.fori_loop(0, per_k, group, 0)

    def finish_chunk(a):
        slot = a % 2
        pltpu.make_async_copy(ebox.at[a, pl.ds(0, tm - 1)], ebox.at[a, pl.ds(0, tm - 1)], end_recv.at[a]).wait()
        enter = jnp.zeros((8, 128), F32)
        for j in range(tm - 1):
            enter = enter + (reach[j, 0] * ebox[a, j] + reach[j, 1] * swap_parts(ebox[a, j]))
        columns = jnp.transpose(jnp.concatenate([enter, jnp.zeros((120, 128), F32)], axis=0))

        for i in range(groups):
            k, t = i // per_k, (i % per_k) * ROW_GROUP
            column = columns[:, i : i + 1].reshape(ROW_GROUP, WIDE, 1)
            r = local[slot, k, t : t + ROW_GROUP]
            growth = grow[k]
            cosine, sine = STEP_WEIGHT * turn[k, 0], STEP_WEIGHT * turn[k, 1]
            r_re = r[:, :ORBITALS] + column[:, :ORBITALS] * growth
            r_im = r[:, ORBITALS:] + column[:, ORBITALS:] * growth
            h_re = (cosine * r_re - sine * r_im).reshape(ROW_GROUP * ORBITALS, 256)
            h_im = (cosine * r_im + sine * r_re).reshape(ROW_GROUP * ORBITALS, 256)
            for h in range(2):
                lanes = slice(128 * h, 128 * h + 128)
                wide[i, h, pl.ds(0, ROW_GROUP * ORBITALS, stride=2), :] = h_re[:, lanes]
                wide[i, h, pl.ds(1, ROW_GROUP * ORBITALS, stride=2), :] = h_im[:, lanes]
                whole = wide[i, h].reshape(ROW_GROUP, WIDE, 128).astype(BF16)
                for e in range(ROW_GROUP):
                    out[k, origin(t + e), field(a), lanes] = whole[e]

    pltpu.make_async_copy(pbox.at[pl.ds(0, tm - 1)], pbox.at[pl.ds(0, tm - 1)], prod_recv).wait()
    through_re, through_im = jnp.ones((8, 128), F32), jnp.zeros((8, 128), F32)
    for j in range(tm - 2, -1, -1):
        p_re, p_im = pbox[j, 0], pbox[j, 1]
        earlier = j < n
        reach[j, 0] = jnp.where(earlier, through_re, 0.0)
        reach[j, 1] = jnp.where(earlier, through_im, 0.0)
        through_re, through_im = (
            jnp.where(earlier, through_re * p_re - through_im * p_im, through_re),
            jnp.where(earlier, through_re * p_im + through_im * p_re, through_im),
        )

    def history(a, carry):
        scan_chunk(a)

        @pl.when(a >= 1)
        def _():
            finish_chunk(a - 1)

        return carry

    lax.fori_loop(0, chunks, history, 0)
    finish_chunk(jnp.int32(chunks - 1))

    def drain(a, carry):
        pltpu.make_async_copy(gh.at[a, pl.ds(0, 4 * mom - 4)], gh.at[a, pl.ds(0, 4 * mom - 4)], fwd_send.at[a]).wait()
        pltpu.make_async_copy(rb.at[a, pl.ds(0, mom - 1)], rb.at[a, pl.ds(0, mom - 1)], ret_send.at[a]).wait()
        pltpu.make_async_copy(ebox.at[a, pl.ds(0, tm - 1)], ebox.at[a, pl.ds(0, tm - 1)], end_send.at[a]).wait()
        return carry

    lax.fori_loop(0, chunks, drain, 0)
    pltpu.make_async_copy(pbox.at[pl.ds(0, tm - 1)], pbox.at[pl.ds(0, tm - 1)], prod_send).wait()


def solution(mesh):
    mom, tm = mesh.shape["mom"], mesh.shape["tm"]

    def shards(green, hole, decay_log, phase_step):
        rows = green.shape[1]
        chunks = ORBITALS
        vmem = pl.BlockSpec(memory_space=pltpu.VMEM)
        anywhere = pl.BlockSpec(memory_space=pl.ANY)
        dma = pltpu.SemaphoreType.DMA
        return pl.pallas_call(
            functools.partial(kernel, mom, tm, rows),
            out_shape=pltpu.VMEM(green.shape, BF16),
            in_specs=[anywhere] * 6,
            out_specs=vmem,
            scratch_shapes=[
                pltpu.VMEM(decay_log.shape, F32),
                pltpu.VMEM(phase_step.shape, F32),
                pltpu.VMEM((2 * MOMENTA, 2 * MOMENTA), BF16),
                pltpu.VMEM((2 * MOMENTA, 2 * MOMENTA), BF16),
                pltpu.VMEM((chunks, 2 * MOMENTA, WIDE, 256), BF16),
                pltpu.VMEM((chunks, MOMENTA, WIDE, 256), BF16),
                pltpu.VMEM((chunks, mom, 2, WIDE, 256), BF16),
                pltpu.VMEM((2, MOMENTA * WIDE, 128), F32),
                pltpu.VMEM((2, MOMENTA * WIDE, 128), F32),
                pltpu.VMEM((2, MOMENTA * WIDE, 128), F32),
                pltpu.VMEM((2, LEVELS, ORBITALS, 256), F32),
                pltpu.VMEM((2, 2, ORBITALS, 256), F32),
                pltpu.VMEM((2, ORBITALS, 256), F32),
                pltpu.VMEM((2, 2 * WIDE, 256), BF16),
                pltpu.VMEM((tm - 1, 2, 8, 128), F32),
                pltpu.VMEM((2, 2, rows, WIDE, 256), F32),
                pltpu.VMEM((2 * rows // ROW_GROUP, 2, ROW_GROUP * WIDE, 128), F32),
                pltpu.VMEM((chunks, 8, 128), F32),
                pltpu.VMEM((chunks, tm, 8, 128), F32),
                pltpu.VMEM((2, 8, 128), F32),
                pltpu.VMEM((tm, 2, 8, 128), F32),
                dma((chunks,)), dma((chunks,)), dma((chunks,)), dma((chunks, rows // ROW_GROUP)),
                dma((chunks,)), dma((chunks,)), dma(()), dma(()), dma((4,)), pltpu.SemaphoreType.REGULAR, pltpu.SemaphoreType.REGULAR,
            ],
            compiler_params=pltpu.CompilerParams(
                collective_id=0, has_side_effects=True, vmem_limit_bytes=56 << 20
            ),
        )(green, hole, decay_log, phase_step, transform_table(1.0), transform_table(-1.0))

    in_specs = (
        P("mom", None, None, "tm"),
        P("mom", None, None, "tm"),
        P("mom", None, "tm"),
        P("mom", None, "tm"),
    )
    out_specs = P("mom", None, None, "tm")
    return jax.shard_map(shards, mesh=mesh, in_specs=in_specs, out_specs=out_specs, check_vma=False)
```

```python
import functools
import math

import jax
import jax.numpy as jnp
import numpy as np
from jax import lax
from jax.experimental import pallas as pl
from jax.experimental.pallas import tpu as pltpu
from jax.sharding import PartitionSpec as P

MESH = pl.DeviceIdType.MESH
F32 = jnp.float32
BF16 = jnp.bfloat16
MOMENTA = 64
ORBITALS = 8
WIDE = 2 * ORBITALS
COUPLING = 0.25
STEP_WEIGHT = 0.0625
LEVELS = 8
ROW_GROUP = 8


def transform_table(handed):
    numbers = np.arange(MOMENTA)
    product = (numbers[:, None] * numbers[None, :]) % MOMENTA
    angles = product.astype(np.float32) * np.float32(2.0 * math.pi / MOMENTA)
    scaled = np.float32(1.0 / math.sqrt(MOMENTA))
    cosine = np.cos(angles) * scaled
    sine = np.float32(handed) * np.sin(angles) * scaled
    return jnp.asarray(np.block([[cosine, -sine], [sine, cosine]]).astype(jnp.bfloat16))


def kernel(
    mom, tm, rows,
    green, hole, decay_in, phase_in, plus_in, minus_in,
    out,
    decay, phase, plus, minus, gh, sb, rb, tg, th, ts, coef, turn, grow, heavy, reach, local, wide,
    est, ebox, pst, pbox,
    fwd_send, fwd_recv, ret_send, ret_recv, end_send, end_recv, prod_send, prod_recv, table_sem, line_z, line_x,
):
    m = lax.axis_index("mom")
    n = lax.axis_index("tm")
    chunks = ORBITALS
    groups = 2 * rows // ROW_GROUP
    per_k = rows // ROW_GROUP
    side = 8
    across = mom // side
    x, z = m // side, m % side

    def offset(j):
        return j // side, j % side

    def target(j):
        dx, dz = offset(j)
        return lax.rem(x + dx, across) * side + lax.rem(z + dz + side, side)

    def origin(j):
        dx, dz = offset(j)
        return lax.rem(x - dx + across, across) * side + lax.rem(z - dz + side, side)

    def field(a):
        return pl.ds(pl.multiple_of(a * WIDE, WIDE), WIDE)

    barrier = pltpu.get_barrier_semaphore()
    ebox[...] = jnp.zeros_like(ebox)
    pbox[...] = jnp.zeros_like(pbox)

    def at(dx, dz):
        return lax.rem(x + dx + across, across) * side + lax.rem(z + dz + side, side)

    def greet(semaphore, **where):
        pl.semaphore_signal(semaphore, inc=1, device_id=where, device_id_type=MESH)

    for dz in (1, -1, 2, -2):
        greet(barrier, mom=at(0, dz))
    for dx in range(1, across):
        greet(barrier, mom=at(dx, 0))

    def greet_tm(j, carry):
        greet(barrier, tm=lax.rem(n + j, tm))
        return carry

    lax.fori_loop(1, tm, greet_tm, 0)
    tables = [
        pltpu.make_async_copy(source, kept, table_sem.at[i])
        for i, (source, kept) in enumerate(
            ((decay_in, decay), (phase_in, phase), (plus_in, plus), (minus_in, minus))
        )
    ]
    for copy in tables:
        copy.start()
    pl.semaphore_wait(barrier, 4 + across - 1 + tm - 1)
    for dz in (2, -2):
        greet(line_z, mom=at(0, dz))

    def send_field(a, j):
        peer = target(j)
        for half, source in enumerate((green, hole)):
            pltpu.make_async_remote_copy(
                src_ref=source.at[:, peer, field(a), :],
                dst_ref=gh.at[a, pl.ds(half * MOMENTA + 2 * m, 2)],
                send_sem=fwd_send.at[a],
                recv_sem=fwd_recv.at[a],
                device_id={"mom": peer},
                device_id_type=MESH,
            ).start()

    def send_near(a, carry):
        for j in (1, side - 1, 2, side - 2):
            send_field(a, j)
        return carry

    def send_far(a, carry):
        for half, source in enumerate((green, hole)):
            pltpu.make_async_copy(
                source.at[:, m, field(a), :],
                gh.at[a, pl.ds(half * MOMENTA + 2 * m, 2)],
                fwd_recv.at[a],
            ).start()

        def one(j, inner):
            @pl.when(jnp.logical_or(j >= side, jnp.logical_and(j > 2, j < side - 2)))
            def _():
                send_field(a, j)

            return inner

        return lax.fori_loop(1, mom, one, carry)

    lax.fori_loop(0, chunks, send_near, 0)
    pl.semaphore_wait(line_z, 2)
    for dx in range(1, across):
        greet(line_x, mom=at(dx, 0))
    pl.semaphore_wait(line_x, across - 1)
    lax.fori_loop(0, chunks, send_far, 0)

    for copy in tables:
        copy.wait()
    lane = lax.broadcasted_iota(jnp.int32, (ORBITALS, 256), 1)
    sub = lax.broadcasted_iota(jnp.int32, (8, 128), 0)
    col = lax.broadcasted_iota(jnp.int32, (8, 128), 1)
    near = lax.broadcasted_iota(jnp.int32, (ROW_GROUP, ORBITALS, 128), 2)
    own_orbital = sub == col % ORBITALS
    real_part = col % WIDE < ORBITALS

    def pattern(column):
        return jnp.sum(jnp.where(own_orbital, column, 0.0), axis=0, keepdims=True)

    def swap_parts(v):
        other = jnp.where(real_part, pltpu.roll(v, 128 - ORBITALS, 1), pltpu.roll(v, ORBITALS, 1))
        return jnp.where(real_part, -other, other)

    last = []
    for k in range(2):
        span = decay[k]
        angle = phase[k]
        for j in range(LEVELS):
            reached = lane >= 2**j
            coef[k, j] = jnp.where(reached, jnp.exp(span), 0.0)
            span = span + jnp.where(reached, pltpu.roll(span, 2**j, 1), 0.0)
            angle = angle + jnp.where(reached, pltpu.roll(angle, 2**j, 1), 0.0)
        cosine, sine, growth = jnp.cos(angle), jnp.sin(angle), jnp.exp(span)
        rest = jnp.where(lane < 255, pltpu.roll(decay[k], 255, 1), 0.0)
        for j in range(LEVELS):
            rest = rest + jnp.where(lane < 256 - 2**j, pltpu.roll(rest, 256 - 2**j, 1), 0.0)
        fade = jnp.exp(rest)
        to_turn = angle[:, 255:256] - angle
        weight = jnp.concatenate([fade * jnp.cos(to_turn), fade * jnp.sin(to_turn)], axis=0)
        high = weight.astype(BF16)
        heavy[k] = jnp.concatenate([high, (weight - high.astype(F32)).astype(BF16)], axis=0)
        turn[k, 0] = cosine
        turn[k, 1] = sine
        grow[k] = growth
        last.append([pattern(v[:, 255:256]) for v in (cosine, sine, growth)])
    first_k = sub < per_k
    end_cos, end_sin, end_grow = (jnp.where(first_k, u, v) for u, v in zip(*last))
    pst[0] = end_grow * end_cos
    pst[1] = end_grow * end_sin

    def send_product(j, carry):
        pltpu.make_async_remote_copy(
            src_ref=pst, dst_ref=pbox.at[n], send_sem=prod_send, recv_sem=prod_recv,
            device_id={"tm": lax.rem(n + j, tm)}, device_id_type=MESH,
        ).start()
        return carry

    lax.fori_loop(1, tm, send_product, 0)

    def work(a, carry):
        pltpu.make_async_copy(gh.at[a], gh.at[a], fwd_recv.at[a]).wait()
        for h in range(2):
            lanes = slice(128 * h, 128 * h + 128)
            tg[h] = gh[a, 0:MOMENTA, :, lanes].astype(F32).reshape(MOMENTA * WIDE, 128)
            th[h] = gh[a, MOMENTA:, :, lanes].astype(F32).reshape(MOMENTA * WIDE, 128)

        def gather(ref, row):
            parts = [
                jnp.concatenate([ref[h, pl.ds(row + c, MOMENTA, stride=WIDE), :] for h in range(2)], axis=1)
                for c in range(2)
            ]
            return jnp.concatenate(parts, axis=0).astype(BF16)

        for b in range(ORBITALS):
            g = jnp.dot(plus[...], gather(tg, 2 * b), preferred_element_type=F32)
            q = jnp.dot(minus[...], gather(th, 2 * b), preferred_element_type=F32)
            g_re, g_im = g[:MOMENTA], g[MOMENTA:]
            q_re, q_im = q[:MOMENTA], q[MOMENTA:]
            square_re = g_re * g_re - g_im * g_im
            square_im = 2.0 * g_re * g_im
            energy_re = COUPLING * (square_re * q_re - square_im * q_im)
            energy_im = COUPLING * (square_re * q_im + square_im * q_re)
            energy = jnp.concatenate([energy_re, energy_im], axis=0).astype(BF16)
            back = jnp.dot(minus[...], energy, preferred_element_type=F32)
            for h in range(2):
                lanes = slice(128 * h, 128 * h + 128)
                for c in range(2):
                    ts[h, pl.ds(c * ORBITALS + b, MOMENTA, stride=WIDE), :] = back[
                        c * MOMENTA : (c + 1) * MOMENTA, lanes
                    ]
        for h in range(2):
            sb[a, :, :, 128 * h : 128 * h + 128] = ts[h].reshape(MOMENTA, WIDE, 128).astype(BF16)

        pltpu.make_async_copy(sb.at[a, pl.ds(2 * m, 2)], rb.at[a, 0], ret_recv.at[a, 0]).start()

        def one(j, inner):
            peer = target(j)
            pltpu.make_async_remote_copy(
                src_ref=sb.at[a, pl.ds(2 * peer, 2)],
                dst_ref=rb.at[a, j],
                send_sem=ret_send.at[a],
                recv_sem=ret_recv.at[a, j // ROW_GROUP],
                device_id={"mom": peer},
                device_id_type=MESH,
            ).start()
            return inner

        return lax.fori_loop(1, mom, one, carry)

    lax.fori_loop(0, chunks, work, 0)

    def scan_chunk(a):
        slot = a % 2

        def ending(q, total):
            t = pl.multiple_of(q * ROW_GROUP, ROW_GROUP)
            block = rb.at[a, pl.ds(t, ROW_GROUP)]
            pltpu.make_async_copy(block, block, ret_recv.at[a, q]).wait()
            for k in range(2):
                v = rb[a, pl.ds(t, ROW_GROUP), k].reshape(ROW_GROUP * WIDE, 256)
                r = lax.dot_general(heavy[k], v, (((1,), (1,)), ((), ())), preferred_element_type=F32)
                r = r[:WIDE] + r[WIDE:]
                p = jnp.sum(jnp.where(own_orbital, r[:ORBITALS], 0.0), axis=0, keepdims=True)
                w = jnp.sum(jnp.where(own_orbital, r[ORBITALS:], 0.0), axis=0, keepdims=True)
                row = p + swap_parts(jnp.broadcast_to(w, (8, 128)))
                total = jnp.where(sub == k * per_k + q, row, total)
            return total

        est[a] = lax.fori_loop(0, per_k, ending, jnp.zeros((8, 128), F32))

        def one(j, carry):
            pltpu.make_async_remote_copy(
                src_ref=est.at[a], dst_ref=ebox.at[a, n], send_sem=end_send.at[a], recv_sem=end_recv.at[a],
                device_id={"tm": lax.rem(n + j, tm)}, device_id_type=MESH,
            ).start()
            return carry

        lax.fori_loop(1, tm, one, 0)

        def group(q, carry):
            t = pl.multiple_of(q * ROW_GROUP, ROW_GROUP)
            for k in range(2):
                v = rb[a, pl.ds(t, ROW_GROUP), k].astype(F32)
                cosine, sine = turn[k, 0], turn[k, 1]
                v_re, v_im = v[:, :ORBITALS], v[:, ORBITALS:]
                y_re = cosine * v_re + sine * v_im
                y_im = cosine * v_im - sine * v_re
                parts = []
                for y in (y_re, y_im):
                    lo, hi = y[:, :, :128], y[:, :, 128:]
                    for j in range(LEVELS - 1):
                        factor = coef[k, j]
                        lo_moved, hi_moved = pltpu.roll(lo, 2**j, 2), pltpu.roll(hi, 2**j, 2)
                        hi = hi + factor[:, 128:] * jnp.where(near >= 2**j, hi_moved, lo_moved)
                        lo = lo + factor[:, :128] * lo_moved
                    hi = hi + coef[k, LEVELS - 1][:, 128:] * lo
                    parts.append((lo, hi))
                los = jnp.concatenate([parts[0][0], parts[1][0]], axis=1)
                his = jnp.concatenate([parts[0][1], parts[1][1]], axis=1)
                local[slot, k, pl.ds(t, ROW_GROUP), :, 0:128] = los
                local[slot, k, pl.ds(t, ROW_GROUP), :, 128:256] = his
            return carry

        lax.fori_loop(0, per_k, group, 0)

    def finish_chunk(a):
        slot = a % 2
        pltpu.make_async_copy(ebox.at[a, pl.ds(0, tm - 1)], ebox.at[a, pl.ds(0, tm - 1)], end_recv.at[a]).wait()
        enter = jnp.zeros((8, 128), F32)
        for j in range(tm - 1):
            enter = enter + (reach[j, 0] * ebox[a, j] + reach[j, 1] * swap_parts(ebox[a, j]))
        columns = jnp.transpose(jnp.concatenate([enter, jnp.zeros((120, 128), F32)], axis=0))

        for i in range(groups):
            k, t = i // per_k, (i % per_k) * ROW_GROUP
            column = columns[:, i : i + 1].reshape(ROW_GROUP, WIDE, 1)
            r = local[slot, k, t : t + ROW_GROUP]
            growth = grow[k]
            cosine, sine = STEP_WEIGHT * turn[k, 0], STEP_WEIGHT * turn[k, 1]
            r_re = r[:, :ORBITALS] + column[:, :ORBITALS] * growth
            r_im = r[:, ORBITALS:] + column[:, ORBITALS:] * growth
            h_re = (cosine * r_re - sine * r_im).reshape(ROW_GROUP * ORBITALS, 256)
            h_im = (cosine * r_im + sine * r_re).reshape(ROW_GROUP * ORBITALS, 256)
            for h in range(2):
                lanes = slice(128 * h, 128 * h + 128)
                wide[i, h, pl.ds(0, ROW_GROUP * ORBITALS, stride=2), :] = h_re[:, lanes]
                wide[i, h, pl.ds(1, ROW_GROUP * ORBITALS, stride=2), :] = h_im[:, lanes]
                whole = wide[i, h].reshape(ROW_GROUP, WIDE, 128).astype(BF16)
                for e in range(ROW_GROUP):
                    out[k, origin(t + e), field(a), lanes] = whole[e]

    pltpu.make_async_copy(pbox.at[pl.ds(0, tm - 1)], pbox.at[pl.ds(0, tm - 1)], prod_recv).wait()
    through_re, through_im = jnp.ones((8, 128), F32), jnp.zeros((8, 128), F32)
    for j in range(tm - 2, -1, -1):
        p_re, p_im = pbox[j, 0], pbox[j, 1]
        earlier = j < n
        reach[j, 0] = jnp.where(earlier, through_re, 0.0)
        reach[j, 1] = jnp.where(earlier, through_im, 0.0)
        through_re, through_im = (
            jnp.where(earlier, through_re * p_re - through_im * p_im, through_re),
            jnp.where(earlier, through_re * p_im + through_im * p_re, through_im),
        )

    def history(a, carry):
        scan_chunk(a)

        @pl.when(a >= 1)
        def _():
            finish_chunk(a - 1)

        return carry

    lax.fori_loop(0, chunks, history, 0)
    finish_chunk(jnp.int32(chunks - 1))

    def drain(a, carry):
        pltpu.make_async_copy(gh.at[a, pl.ds(0, 4 * mom - 4)], gh.at[a, pl.ds(0, 4 * mom - 4)], fwd_send.at[a]).wait()
        pltpu.make_async_copy(rb.at[a, pl.ds(0, mom - 1)], rb.at[a, pl.ds(0, mom - 1)], ret_send.at[a]).wait()
        pltpu.make_async_copy(ebox.at[a, pl.ds(0, tm - 1)], ebox.at[a, pl.ds(0, tm - 1)], end_send.at[a]).wait()
        return carry

    lax.fori_loop(0, chunks, drain, 0)
    pltpu.make_async_copy(pbox.at[pl.ds(0, tm - 1)], pbox.at[pl.ds(0, tm - 1)], prod_send).wait()


def solution(mesh):
    mom, tm = mesh.shape["mom"], mesh.shape["tm"]

    def shards(green, hole, decay_log, phase_step):
        rows = green.shape[1]
        chunks = ORBITALS
        vmem = pl.BlockSpec(memory_space=pltpu.VMEM)
        anywhere = pl.BlockSpec(memory_space=pl.ANY)
        dma = pltpu.SemaphoreType.DMA
        return pl.pallas_call(
            functools.partial(kernel, mom, tm, rows),
            out_shape=pltpu.VMEM(green.shape, BF16),
            in_specs=[anywhere] * 6,
            out_specs=vmem,
            scratch_shapes=[
                pltpu.VMEM(decay_log.shape, F32),
                pltpu.VMEM(phase_step.shape, F32),
                pltpu.VMEM((2 * MOMENTA, 2 * MOMENTA), BF16),
                pltpu.VMEM((2 * MOMENTA, 2 * MOMENTA), BF16),
                pltpu.VMEM((chunks, 2 * MOMENTA, WIDE, 256), BF16),
                pltpu.VMEM((chunks, MOMENTA, WIDE, 256), BF16),
                pltpu.VMEM((chunks, mom, 2, WIDE, 256), BF16),
                pltpu.VMEM((2, MOMENTA * WIDE, 128), F32),
                pltpu.VMEM((2, MOMENTA * WIDE, 128), F32),
                pltpu.VMEM((2, MOMENTA * WIDE, 128), F32),
                pltpu.VMEM((2, LEVELS, ORBITALS, 256), F32),
                pltpu.VMEM((2, 2, ORBITALS, 256), F32),
                pltpu.VMEM((2, ORBITALS, 256), F32),
                pltpu.VMEM((2, 2 * WIDE, 256), BF16),
                pltpu.VMEM((tm - 1, 2, 8, 128), F32),
                pltpu.VMEM((2, 2, rows, WIDE, 256), F32),
                pltpu.VMEM((2 * rows // ROW_GROUP, 2, ROW_GROUP * WIDE, 128), F32),
                pltpu.VMEM((chunks, 8, 128), F32),
                pltpu.VMEM((chunks, tm, 8, 128), F32),
                pltpu.VMEM((2, 8, 128), F32),
                pltpu.VMEM((tm, 2, 8, 128), F32),
                dma((chunks,)), dma((chunks,)), dma((chunks,)), dma((chunks, rows // ROW_GROUP)),
                dma((chunks,)), dma((chunks,)), dma(()), dma(()), dma((4,)), pltpu.SemaphoreType.REGULAR, pltpu.SemaphoreType.REGULAR,
            ],
            compiler_params=pltpu.CompilerParams(
                collective_id=0, has_side_effects=True, vmem_limit_bytes=56 << 20
            ),
        )(green, hole, decay_log, phase_step, transform_table(1.0), transform_table(-1.0))

    in_specs = (
        P("mom", None, None, "tm"),
        P("mom", None, None, "tm"),
        P("mom", None, "tm"),
        P("mom", None, "tm"),
    )
    out_specs = P("mom", None, None, "tm")
    return jax.shard_map(shards, mesh=mesh, in_specs=in_specs, out_specs=out_specs, check_vma=False)
```
